128 devices in a mesh: tm: 8 (over y, x_hi), nrn: 16 (over x_lo, z, core).
Axes of the slice: x: 4 (x_hi: 2, x_lo: 2; x = x_hi * 2 + x_lo), y: 4, z: 4, core: 2. Of those that a mesh axis runs over, the one named last changes fastest.
Arguments:
- spikes: bfloat16 [32768, 32768], P('tm', 'nrn'), may hold values from -6 to 6
- read_in: bfloat16 [32768, 128], P('nrn'), may hold values from -0.03125 to 0.03125
- kernel: float32 [128, 32768], P(('tm', 'nrn')), may hold values from -0.03125 to 0.03125
- gain: float32 [128], replicated, may hold values from 0.1 to 1.9
- w_gate: bfloat16 [128, 512], replicated, may hold values from -0.5 to 0.5
- w_up: bfloat16 [128, 512], replicated, may hold values from -0.5 to 0.5
- w_down: bfloat16 [512, 128], replicated, may hold values from -0.25 to 0.25
Outputs:
- denoised: bfloat16 [32768, 128], P(('tm', 'nrn'))
The draws below stay inside these ranges and needn't reach their ends.
All inputs are finite; a program needn't handle non-finite values.
Results may differ from the reference program's by a relative error of at most 0.0045.
Values sent between devices are 32-bit elements; how exact they have to be, the bound alone decides.
No kernel may reach another device: no remote copies, remote signals or barrier semaphores. Data moves between devices by JAX's collectives and lax.ppermute only.
A program may use at most 64 MiB of HBM per device.

```python
import jax
import jax.numpy as jnp
from jax import lax

NEURONS = 32768
LATENT = 128
HIDDEN_SIZE = 512
TIME = 32768


def block_scale(stream_key, extent, cuts, smallest, largest):
    def one(position, blocks):
        draws = jax.random.uniform(jax.random.fold_in(jax.random.fold_in(stream_key, 6), position), (blocks,), jnp.float32, smallest / len(cuts), largest / len(cuts))
        return jnp.repeat(jnp.exp(draws), extent[position] // blocks).reshape((-1,) + (1,) * (len(extent) - position - 1))

    level = one(*cuts[0])
    for cut in cuts[1:]:
        level = level * one(*cut)
    return level


def bell_draw(key, extent, deviation, most, pieces=(), held_as=jnp.bfloat16):
    result = deviation * jax.random.normal(key, extent, jnp.float32)
    if pieces:
        result = result * block_scale(key, extent, pieces, -0.22, 0.18)
    return jnp.clip(result, -most, most).astype(held_as)


def setup_inputs(seed: int = 0) -> dict:
    keys = jax.random.split(jax.random.key(seed), 8)
    return {
        "spikes": bell_draw(keys[0], (TIME, NEURONS), 1.0, 6.0, ((0, 8), (1, 16))),
        "read_in": bell_draw(keys[1], (NEURONS, LATENT), NEURONS ** -0.5, 0.03125, ((0, 16),)),
        "kernel": bell_draw(keys[2], (LATENT, TIME), TIME ** -0.5, 0.03125, ((0, 128),), jnp.float32),
        "gain": jnp.clip(1.0 + 0.18 * jax.random.normal(keys[3], (LATENT,), jnp.float32), 0.1, 1.9),
        "w_gate": bell_draw(keys[4], (LATENT, HIDDEN_SIZE), LATENT ** -0.5, 0.5),
        "w_up": bell_draw(keys[5], (LATENT, HIDDEN_SIZE), LATENT ** -0.5, 0.5),
        "w_down": bell_draw(keys[6], (HIDDEN_SIZE, LATENT), HIDDEN_SIZE ** -0.5, 0.25),
    }


def reference(spikes, read_in, kernel, gain, w_gate, w_up, w_down):
    latent = jnp.dot(spikes, read_in, preferred_element_type=jnp.float32)
    spectrum = jnp.fft.fft(latent.T, axis=-1) * jnp.fft.fft(kernel, axis=-1)
    conv = jnp.fft.ifft(spectrum, axis=-1).real.astype(jnp.float32).T
    mixed = latent + conv
    meansq = lax.optimization_barrier(jnp.mean(mixed * mixed, axis=-1, keepdims=True))
    normed = (mixed * jax.lax.rsqrt(meansq + 1e-05) * gain).astype(jnp.bfloat16)
    gate = jnp.dot(normed, w_gate, preferred_element_type=jnp.float32)
    upper = jnp.dot(normed, w_up, preferred_element_type=jnp.float32)
    act = (jax.nn.silu(gate) * upper).astype(jnp.bfloat16)
    return (mixed + jnp.dot(act, w_down, preferred_element_type=jnp.float32)).astype(jnp.bfloat16)
```

```python
import math

import jax
import jax.numpy as jnp
import numpy as np
from jax import lax
from jax.experimental import pallas as pl
from jax.experimental.pallas import tpu as pltpu
from jax.sharding import PartitionSpec as P

f32 = jnp.float32
bf16 = jnp.bfloat16
LANES = 128


def split(table):
    table = np.asarray(table, np.float32)
    high = table.astype(jnp.bfloat16)
    low = (table - high.astype(np.float32)).astype(jnp.bfloat16)
    return jnp.asarray(high), jnp.asarray(low)


def dft_tables(rows):
    half = rows // 2 + 1
    padded = -(-half // 8) * 8
    total = rows * LANES
    a = np.arange(padded)
    keep = (a < half).astype(np.float64)
    row = np.arange(rows)
    angle = 2 * math.pi * ((a[:, None] * row[None, :]) % rows) / rows
    first = np.concatenate([np.cos(angle), -np.sin(angle)]) * np.tile(keep, 2)[:, None]
    lane = np.arange(LANES)
    angle = 2 * math.pi * ((a[:, None] * lane[None, :]) % total) / total
    twist_cos, twist_sin = np.cos(angle), np.sin(angle)
    angle = 2 * math.pi * ((lane[:, None] * lane[None, :]) % LANES) / LANES
    cos, sin = np.cos(angle), np.sin(angle)
    second = np.block([[cos, -sin], [sin, cos]])
    third = np.block([[cos, sin], [-sin, cos]])
    weight = np.where((a == 0) | (a == rows // 2), 1.0, 2.0) * keep
    angle = 2 * math.pi * ((row[:, None] * a[None, :]) % rows) / rows
    fourth = np.concatenate([np.cos(angle) * weight, -np.sin(angle) * weight], axis=1)
    return padded, first, twist_cos, twist_sin, second, third, fourth


def triple(left, right):
    (lh, ll), (rh, rl) = left, right
    dot = lambda p, q: jnp.dot(p, q, preferred_element_type=f32)
    return dot(lh, rh) + (dot(lh, rl) + dot(ll, rh))


def halves(value):
    high = value.astype(bf16)
    return high, (value - high.astype(f32)).astype(bf16)


def forward(signal, refs, padded):
    first_h, first_l, tc, ts, second_h, second_l = refs
    outer = triple((first_h[...], first_l[...]), halves(signal))
    real, imag = outer[:padded], outer[padded:]
    cos, sin = tc[...], ts[...]
    turned = jnp.concatenate([real * cos + imag * sin, imag * cos - real * sin], axis=1)
    return triple(halves(turned), (second_h[...], second_l[...]))


def project_kernel(core_ref, spikes_ref, read_ref, own_ref, other_ref, weight_ref):
    step = pl.program_id(0)
    width = read_ref.shape[1]

    @pl.when(step == 0)
    def _():
        channel = lax.broadcasted_iota(jnp.int32, (width, width), 0)
        place = lax.broadcasted_iota(jnp.int32, (width, width), 1)
        half = width // 2
        late = (place >= half).astype(jnp.int32)
        core = core_ref[0]
        wanted = 2 * (place - half * late) + (core + late - 2 * core * late)
        pick = jnp.where(channel == wanted, 1.0, 0.0).astype(bf16)
        weight_ref[...] = jnp.dot(read_ref[...], pick, preferred_element_type=f32).astype(bf16)

    part = jnp.dot(spikes_ref[...], weight_ref[...], preferred_element_type=f32)
    rows = part.shape[0] // LANES
    half = width // 2
    for k in range(rows):
        block = part[k * LANES : (k + 1) * LANES].T
        own_ref[:, step * rows + k, :] = block[:half]
        other_ref[:, step * rows + k, :] = block[half:]


def project(core, spikes, read_in, block):
    bins, neurons = spikes.shape
    width = read_in.shape[1]
    out = jax.ShapeDtypeStruct((width // 2, bins // LANES, LANES), f32)
    full = pl.BlockSpec(out.shape, lambda i, c: (0, 0, 0))
    return pl.pallas_call(
        project_kernel,
        out_shape=(out, out),
        grid_spec=pltpu.PrefetchScalarGridSpec(
            num_scalar_prefetch=1,
            grid=(bins // block,),
            in_specs=[
                pl.BlockSpec((block, neurons), lambda i, c: (i, 0)),
                pl.BlockSpec((neurons, width), lambda i, c: (0, 0)),
            ],
            out_specs=(full, full),
            scratch_shapes=[pltpu.VMEM((neurons, width), bf16)],
        ),
        compiler_params=pltpu.CompilerParams(
            dimension_semantics=("arbitrary",), vmem_limit_bytes=40 << 20
        ),
        name="project",
    )(core, spikes, read_in)


def spectrum_kernel(kern_ref, fh, fl, tc, ts, sh, sl, out_ref, *, padded, scale):
    out_ref[...] = forward(kern_ref[...], (fh, fl, tc, ts, sh, sl), padded) * scale


def convolve_kernel(
    parts_ref, spec_ref, fh, fl, tc, ts, sh, sl, th, tl, gh, gl, out_ref, *, padded, groups
):
    parts = parts_ref[...]
    each, lanes = parts.shape[1], parts.shape[2]
    members = parts.shape[0] // groups
    parts = parts.reshape(groups, members, each, lanes)
    series = parts[:, 0]
    for m in range(1, members):
        series = series + parts[:, m]
    series = series.reshape(groups * each, lanes)
    data = forward(series, (fh, fl, tc, ts, sh, sl), padded)
    dr, di = data[:, :LANES], data[:, LANES:]
    spec = spec_ref[...]
    kr, ki = spec[:, :LANES], spec[:, LANES:]
    prod = jnp.concatenate([dr * kr - di * ki, dr * ki + di * kr], axis=1)
    back = triple(halves(prod), (th[...], tl[...]))
    br, bi = back[:, :LANES], back[:, LANES:]
    cos, sin = tc[...], ts[...]
    turned = jnp.concatenate([br * cos - bi * sin, br * sin + bi * cos], axis=0)
    out_ref[...] = series + triple((gh[...], gl[...]), halves(turned))


def mlp_kernel(stack_ref, gain_ref, gate_ref, up_ref, down_ref, out_ref):
    channels = gate_ref.shape[0]
    each = stack_ref.shape[0] // channels
    residual = jnp.concatenate(
        [stack_ref[pl.ds(r, channels, stride=each), :].T for r in range(each)], axis=0
    )
    meansq = jnp.mean(residual * residual, axis=-1, keepdims=True)
    normed = (residual * lax.rsqrt(meansq + 1e-05) * gain_ref[...]).astype(bf16)
    gate = jnp.dot(normed, gate_ref[...], preferred_element_type=f32)
    upper = jnp.dot(normed, up_ref[...], preferred_element_type=f32)
    act = (gate / (1.0 + jnp.exp(-gate)) * upper).astype(bf16)
    out_ref[...] = (
        residual + jnp.dot(act, down_ref[...], preferred_element_type=f32)
    ).astype(bf16)


def per_device(spikes, read_in, kernel, gain, w_gate, w_up, w_down):
    time_groups = lax.axis_size("tm")
    neuron_groups = lax.axis_size("nrn")
    devices = time_groups * neuron_groups
    session = spikes.shape[0] * time_groups
    rows = session // LANES
    padded, first, twist_cos, twist_sin, second, third, fourth = dft_tables(rows)
    twist = (jnp.asarray(twist_cos, f32), jnp.asarray(twist_sin, f32))
    ahead = (*split(first), *twist, *split(second))
    core = (lax.axis_index("nrn") % 2).astype(jnp.int32).reshape(1)
    own, other = project(core, spikes, read_in, 512)
    swapped = lax.ppermute(other, "nrn", [(j, j ^ 1) for j in range(neuron_groups)])
    same = [[d for d in range(devices) if d % 2 == c] for c in range(2)]
    parts = lax.all_to_all(
        own + swapped, ("tm", "nrn"), 0, 0, tiled=True, axis_index_groups=same
    )
    spec = pl.pallas_call(
        lambda *refs: spectrum_kernel(*refs, padded=padded, scale=1.0 / session),
        out_shape=jax.ShapeDtypeStruct((padded, 2 * LANES), f32),
        name="spectrum",
    )(kernel.reshape(rows, LANES), *ahead)
    mixed = pl.pallas_call(
        lambda *refs: convolve_kernel(*refs, padded=padded, groups=time_groups),
        out_shape=jax.ShapeDtypeStruct((rows, LANES), f32),
        compiler_params=pltpu.CompilerParams(vmem_limit_bytes=40 << 20),
        name="convolve",
    )(parts, spec, *ahead, *split(third), *split(fourth))
    stacked = lax.all_to_all(
        mixed.reshape(devices, rows // devices, LANES), ("tm", "nrn"), 0, 0, tiled=True
    )
    return pl.pallas_call(
        mlp_kernel,
        out_shape=jax.ShapeDtypeStruct((rows * LANES // devices, gain.shape[0]), bf16),
        name="mlp",
    )(stacked.reshape(rows, LANES), gain.reshape(1, -1), w_gate, w_up, w_down)


def solution(mesh):
    placed = (P("tm", "nrn"), P("nrn", None), P(("tm", "nrn"), None), P(), P(), P(), P())
    return jax.shard_map(
        per_device, mesh=mesh, in_specs=placed, out_specs=P(("tm", "nrn"), None), check_vma=False
    )
```

```python
import math

import jax
import jax.numpy as jnp
import numpy as np
from jax import lax
from jax.experimental import pallas as pl
from jax.experimental.pallas import tpu as pltpu
from jax.sharding import PartitionSpec as P

f32 = jnp.float32
bf16 = jnp.bfloat16
LANES = 128


def split(table):
    table = np.asarray(table, np.float32)
    high = table.astype(jnp.bfloat16)
    low = (table - high.astype(np.float32)).astype(jnp.bfloat16)
    return jnp.asarray(high), jnp.asarray(low)


def dft_tables(rows):
    half = rows // 2 + 1
    padded = -(-half // 8) * 8
    total = rows * LANES
    a = np.arange(padded)
    keep = (a < half).astype(np.float64)
    row = np.arange(rows)
    angle = 2 * math.pi * ((a[:, None] * row[None, :]) % rows) / rows
    first = np.concatenate([np.cos(angle), -np.sin(angle)]) * np.tile(keep, 2)[:, None]
    lane = np.arange(LANES)
    angle = 2 * math.pi * ((a[:, None] * lane[None, :]) % total) / total
    twist_cos, twist_sin = np.cos(angle), np.sin(angle)
    angle = 2 * math.pi * ((lane[:, None] * lane[None, :]) % LANES) / LANES
    cos, sin = np.cos(angle), np.sin(angle)
    second = np.block([[cos, -sin], [sin, cos]])
    third = np.block([[cos, sin], [-sin, cos]])
    weight = np.where((a == 0) | (a == rows // 2), 1.0, 2.0) * keep
    angle = 2 * math.pi * ((row[:, None] * a[None, :]) % rows) / rows
    fourth = np.concatenate([np.cos(angle) * weight, -np.sin(angle) * weight], axis=1)
    return padded, first, twist_cos, twist_sin, second, third, fourth


def triple(left, right):
    (lh, ll), (rh, rl) = left, right
    dot = lambda p, q: jnp.dot(p, q, preferred_element_type=f32)
    return dot(lh, rh) + (dot(lh, rl) + dot(ll, rh))


def halves(value):
    high = value.astype(bf16)
    return high, (value - high.astype(f32)).astype(bf16)


def forward(signal, refs, padded):
    first_h, first_l, tc, ts, second_h, second_l = refs
    outer = triple((first_h[...], first_l[...]), halves(signal))
    real, imag = outer[:padded], outer[padded:]
    cos, sin = tc[...], ts[...]
    turned = jnp.concatenate([real * cos + imag * sin, imag * cos - real * sin], axis=1)
    return triple(halves(turned), (second_h[...], second_l[...]))


def project_kernel(core_ref, spikes_hbm, read_hbm, own_ref, other_ref, *scratch, pieces):
    spikes_ref, read_ref, weight_ref, arrived, read_arrived = scratch
    width = read_ref.shape[1]
    half = width // 2
    starts = [sum(pieces[:i]) for i in range(len(pieces))]
    fetch_read = pltpu.make_async_copy(read_hbm, read_ref, read_arrived)
    fetch_read.start()
    fetches = [
        pltpu.make_async_copy(
            spikes_hbm.at[pl.ds(first, size)], spikes_ref.at[pl.ds(first, size)], arrived.at[i]
        )
        for i, (first, size) in enumerate(zip(starts, pieces))
    ]
    for fetch in fetches[:2]:
        fetch.start()
    fetch_read.wait()
    channel = lax.broadcasted_iota(jnp.int32, (width, width), 0)
    place = lax.broadcasted_iota(jnp.int32, (width, width), 1)
    late = (place >= half).astype(jnp.int32)
    core = core_ref[0]
    wanted = 2 * (place - half * late) + (core + late - 2 * core * late)
    pick = jnp.where(channel == wanted, 1.0, 0.0).astype(bf16)
    weight_ref[...] = jnp.dot(read_ref[...], pick, preferred_element_type=f32).astype(bf16)

    def put(part, block):
        turned = part.T
        own_ref[:, block, :] = turned[:half]
        other_ref[:, block, :] = turned[half:]

    held = None
    for i, (first, size) in enumerate(zip(starts, pieces)):
        fetches[i].wait()
        if i + 2 < len(pieces):
            fetches[i + 2].start()
        for row in range(first, first + size, LANES):
            part = jnp.dot(
                spikes_ref[pl.ds(row, LANES)], weight_ref[...], preferred_element_type=f32
            )
            if held is not None:
                put(*held)
            held = (part, row // LANES)
    put(*held)


def project(core, spikes, read_in):
    bins, neurons = spikes.shape
    width = read_in.shape[1]
    out = jax.ShapeDtypeStruct((width // 2, bins // LANES, LANES), f32)
    pieces = [bins // 8] + [bins // 4] * 3 + [bins // 8]
    return pl.pallas_call(
        lambda *refs: project_kernel(*refs, pieces=pieces),
        out_shape=(out, out),
        in_specs=[
            pl.BlockSpec(memory_space=pltpu.SMEM),
            pl.BlockSpec(memory_space=pltpu.HBM),
            pl.BlockSpec(memory_space=pltpu.HBM),
        ],
        scratch_shapes=[
            pltpu.VMEM((bins, neurons), bf16),
            pltpu.VMEM((neurons, width), bf16),
            pltpu.VMEM((neurons, width), bf16),
            pltpu.SemaphoreType.DMA((len(pieces),)),
            pltpu.SemaphoreType.DMA,
        ],
        compiler_params=pltpu.CompilerParams(vmem_limit_bytes=24 << 20),
        name="project",
    )(core, spikes, read_in)


def spectrum_kernel(kern_ref, fh, fl, tc, ts, sh, sl, out_ref, *, padded, scale):
    out_ref[...] = forward(kern_ref[...], (fh, fl, tc, ts, sh, sl), padded) * scale


def convolve_kernel(
    parts_ref, spec_ref, fh, fl, tc, ts, sh, sl, th, tl, gh, gl, out_ref, *, padded, groups
):
    parts = parts_ref[...]
    each, lanes = parts.shape[1], parts.shape[2]
    members = parts.shape[0] // groups
    parts = parts.reshape(groups, members, each, lanes)
    series = parts[:, 0]
    for m in range(1, members):
        series = series + parts[:, m]
    series = series.reshape(groups * each, lanes)
    data = forward(series, (fh, fl, tc, ts, sh, sl), padded)
    dr, di = data[:, :LANES], data[:, LANES:]
    spec = spec_ref[...]
    kr, ki = spec[:, :LANES], spec[:, LANES:]
    prod = jnp.concatenate([dr * kr - di * ki, dr * ki + di * kr], axis=1)
    back = triple(halves(prod), (th[...], tl[...]))
    br, bi = back[:, :LANES], back[:, LANES:]
    cos, sin = tc[...], ts[...]
    turned = jnp.concatenate([br * cos - bi * sin, br * sin + bi * cos], axis=0)
    out_ref[...] = series + triple((gh[...], gl[...]), halves(turned))


def mlp_kernel(stack_ref, gain_ref, gate_ref, up_ref, down_ref, out_ref):
    channels = gate_ref.shape[0]
    each = stack_ref.shape[0] // channels
    residual = jnp.concatenate(
        [stack_ref[pl.ds(r, channels, stride=each), :].T for r in range(each)], axis=0
    )
    meansq = jnp.mean(residual * residual, axis=-1, keepdims=True)
    normed = (residual * lax.rsqrt(meansq + 1e-05) * gain_ref[...]).astype(bf16)
    gate = jnp.dot(normed, gate_ref[...], preferred_element_type=f32)
    upper = jnp.dot(normed, up_ref[...], preferred_element_type=f32)
    act = (gate / (1.0 + jnp.exp(-gate)) * upper).astype(bf16)
    out_ref[...] = (
        residual + jnp.dot(act, down_ref[...], preferred_element_type=f32)
    ).astype(bf16)


def per_device(spikes, read_in, kernel, gain, w_gate, w_up, w_down):
    time_groups = lax.axis_size("tm")
    neuron_groups = lax.axis_size("nrn")
    devices = time_groups * neuron_groups
    session = spikes.shape[0] * time_groups
    rows = session // LANES
    padded, first, twist_cos, twist_sin, second, third, fourth = dft_tables(rows)
    twist = (jnp.asarray(twist_cos, f32), jnp.asarray(twist_sin, f32))
    ahead = (*split(first), *twist, *split(second))
    core = (lax.axis_index("nrn") % 2).astype(jnp.int32).reshape(1)
    spikes, read_in = (
        pltpu.with_memory_space_constraint(x, pltpu.HBM) for x in (spikes, read_in)
    )
    own, other = project(core, spikes, read_in)
    swapped = lax.ppermute(other, "nrn", [(j, j ^ 1) for j in range(neuron_groups)])
    spec = pl.pallas_call(
        lambda *refs: spectrum_kernel(*refs, padded=padded, scale=1.0 / session),
        out_shape=jax.ShapeDtypeStruct((padded, 2 * LANES), f32),
        compiler_params=pltpu.CompilerParams(vmem_limit_bytes=8 << 20),
        name="spectrum",
    )(kernel.reshape(rows, LANES), *ahead)
    swapped, spec = lax.optimization_barrier((swapped, spec))
    same = [[d for d in range(devices) if d % 2 == c] for c in range(2)]
    parts = lax.all_to_all(
        own + swapped, ("tm", "nrn"), 0, 0, tiled=True, axis_index_groups=same
    )
    mixed = pl.pallas_call(
        lambda *refs: convolve_kernel(*refs, padded=padded, groups=time_groups),
        out_shape=jax.ShapeDtypeStruct((rows, LANES), f32),
        compiler_params=pltpu.CompilerParams(vmem_limit_bytes=12 << 20),
        name="convolve",
    )(parts, spec, *ahead, *split(third), *split(fourth))
    stacked = lax.all_to_all(
        mixed.reshape(devices, rows // devices, LANES), ("tm", "nrn"), 0, 0, tiled=True
    )
    return pl.pallas_call(
        mlp_kernel,
        out_shape=jax.ShapeDtypeStruct((rows * LANES // devices, gain.shape[0]), bf16),
        compiler_params=pltpu.CompilerParams(vmem_limit_bytes=12 << 20),
        name="mlp",
    )(stacked.reshape(rows, LANES), gain.reshape(1, -1), w_gate, w_up, w_down)


def solution(mesh):
    placed = (P("tm", "nrn"), P("nrn", None), P(("tm", "nrn"), None), P(), P(), P(), P())
    return jax.shard_map(
        per_device, mesh=mesh, in_specs=placed, out_specs=P(("tm", "nrn"), None), check_vma=False
    )
```

```python
import math

import jax
import jax.numpy as jnp
import numpy as np
from jax import lax
from jax.experimental import pallas as pl
from jax.experimental.pallas import tpu as pltpu
from jax.sharding import PartitionSpec as P

f32 = jnp.float32
bf16 = jnp.bfloat16
LANES = 128


def split(table):
    table = np.asarray(table, np.float32)
    high = table.astype(jnp.bfloat16)
    low = (table - high.astype(np.float32)).astype(jnp.bfloat16)
    return jnp.asarray(high), jnp.asarray(low)


def dft_tables(rows):
    half = rows // 2 + 1
    padded = -(-half // 8) * 8
    total = rows * LANES
    a = np.arange(padded)
    keep = (a < half).astype(np.float64)
    row = np.arange(rows)
    angle = 2 * math.pi * ((a[:, None] * row[None, :]) % rows) / rows
    first = np.concatenate([np.cos(angle), -np.sin(angle)]) * np.tile(keep, 2)[:, None]
    lane = np.arange(LANES)
    angle = 2 * math.pi * ((a[:, None] * lane[None, :]) % total) / total
    twist_cos, twist_sin = np.cos(angle), np.sin(angle)
    angle = 2 * math.pi * ((lane[:, None] * lane[None, :]) % LANES) / LANES
    cos, sin = np.cos(angle), np.sin(angle)
    second = np.block([[cos, -sin], [sin, cos]])
    third = np.block([[cos, sin], [-sin, cos]])
    weight = np.where((a == 0) | (a == rows // 2), 1.0, 2.0) * keep
    angle = 2 * math.pi * ((row[:, None] * a[None, :]) % rows) / rows
    fourth = np.concatenate([np.cos(angle) * weight, -np.sin(angle) * weight], axis=1)
    return padded, first, twist_cos, twist_sin, second, third, fourth


def triple(left, right):
    (lh, ll), (rh, rl) = left, right
    dot = lambda p, q: jnp.dot(p, q, preferred_element_type=f32)
    return dot(lh, rh) + (dot(lh, rl) + dot(ll, rh))


def halves(value):
    high = value.astype(bf16)
    return high, (value - high.astype(f32)).astype(bf16)


def forward(signal, refs, padded):
    first_h, first_l, tc, ts, second_h, second_l = refs
    outer = triple((first_h[...], first_l[...]), halves(signal))
    real, imag = outer[:padded], outer[padded:]
    cos, sin = tc[...], ts[...]
    turned = jnp.concatenate([real * cos + imag * sin, imag * cos - real * sin], axis=1)
    return triple(halves(turned), (second_h[...], second_l[...]))


def put(part, own_ref, other_ref, block):
    turned = part.T
    half = turned.shape[0] // 2
    own_ref[:, block, :] = turned[:half]
    other_ref[:, block, :] = turned[half:]


def products(spikes_ref, weight, rows, own_ref, other_ref, held):
    for row in rows:
        part = jnp.dot(spikes_ref[pl.ds(row, LANES)], weight[...], preferred_element_type=f32)
        if held is not None:
            put(held[0], own_ref, other_ref, held[1])
        held = (part, row // LANES)
    return held


def project_kernel(core_ref, spikes_hbm, read_hbm, own_ref, other_ref, rest_ref, weight_ref, *scratch, pieces):
    spikes_ref, read_ref, arrived, read_arrived = scratch
    width = read_ref.shape[1]
    half = width // 2
    starts = [sum(pieces[:i]) for i in range(len(pieces) + 1)]
    fetch_read = pltpu.make_async_copy(read_hbm, read_ref, read_arrived)
    fetch_read.start()
    fetches = [
        pltpu.make_async_copy(
            spikes_hbm.at[pl.ds(first, size)], spikes_ref.at[pl.ds(first, size)], arrived.at[i]
        )
        for i, (first, size) in enumerate(zip(starts, pieces))
    ]
    fetches.append(
        pltpu.make_async_copy(
            spikes_hbm.at[pl.ds(starts[-1], rest_ref.shape[0])], rest_ref, arrived.at[len(pieces)]
        )
    )
    for fetch in fetches[:2]:
        fetch.start()
    fetch_read.wait()
    channel = lax.broadcasted_iota(jnp.int32, (width, width), 0)
    place = lax.broadcasted_iota(jnp.int32, (width, width), 1)
    late = (place >= half).astype(jnp.int32)
    core = core_ref[0]
    wanted = 2 * (half - 1 - (place - half * late)) + (core + late - 2 * core * late)
    pick = jnp.where(channel == wanted, 1.0, 0.0).astype(bf16)
    weight_ref[...] = jnp.dot(read_ref[...], pick, preferred_element_type=f32).astype(bf16)
    held = None
    for i, (first, size) in enumerate(zip(starts, pieces)):
        fetches[i].wait()
        if i + 2 < len(fetches):
            fetches[i + 2].start()
        rows = range(first, first + size, LANES)
        held = products(spikes_ref, weight_ref, rows, own_ref, other_ref, held)
    put(held[0], own_ref, other_ref, held[1])
    fetches[-1].wait()


def rest_kernel(rest_ref, weight_ref, own_ref, other_ref):
    rows = range(0, rest_ref.shape[0], LANES)
    held = products(rest_ref, weight_ref, rows, own_ref, other_ref, None)
    put(held[0], own_ref, other_ref, held[1])


def project(core, spikes, read_in, swap):
    bins, neurons = spikes.shape
    width = read_in.shape[1]
    part = lambda rows: jax.ShapeDtypeStruct((width // 2, rows // LANES, LANES), f32)
    pieces = [bins // 8, bins // 4, bins // 4, bins // 8]
    head = sum(pieces)
    tail = bins - head
    vmem = pl.BlockSpec(memory_space=pltpu.VMEM)
    own, other, rest, weight = pl.pallas_call(
        lambda *refs: project_kernel(*refs, pieces=pieces),
        out_shape=(
            part(head),
            part(head),
            jax.ShapeDtypeStruct((tail, neurons), bf16),
            jax.ShapeDtypeStruct((neurons, width), bf16),
        ),
        in_specs=[
            pl.BlockSpec(memory_space=pltpu.SMEM),
            pl.BlockSpec(memory_space=pltpu.HBM),
            pl.BlockSpec(memory_space=pltpu.HBM),
        ],
        out_specs=(vmem,) * 4,
        scratch_shapes=[
            pltpu.VMEM((head, neurons), bf16),
            pltpu.VMEM((neurons, width), bf16),
            pltpu.SemaphoreType.DMA((len(pieces) + 1,)),
            pltpu.SemaphoreType.DMA,
        ],
        compiler_params=pltpu.CompilerParams(vmem_limit_bytes=24 << 20),
        name="project",
    )(core, spikes, read_in)
    swapped = swap(other)
    own_rest, other_rest = pl.pallas_call(
        rest_kernel,
        out_shape=(part(tail), part(tail)),
        compiler_params=pltpu.CompilerParams(vmem_limit_bytes=8 << 20),
        name="rest",
    )(rest, weight)
    return own, swapped, own_rest, swap(other_rest)


def spectrum_kernel(kern_ref, fh, fl, tc, ts, sh, sl, out_ref, *, padded, scale):
    out_ref[...] = forward(kern_ref[...], (fh, fl, tc, ts, sh, sl), padded) * scale


def convolve_kernel(
    parts_ref, spec_ref, fh, fl, tc, ts, sh, sl, th, tl, gh, gl, out_ref, *, padded, groups
):
    parts = parts_ref[...]
    each, lanes = parts.shape[1], parts.shape[2]
    members = parts.shape[0] // groups
    parts = parts.reshape(groups, members, each, lanes)
    series = parts[:, 0]
    for m in range(1, members):
        series = series + parts[:, m]
    series = jnp.concatenate([series[g] for g in reversed(range(groups))], axis=0)
    data = forward(series, (fh, fl, tc, ts, sh, sl), padded)
    dr, di = data[:, :LANES], data[:, LANES:]
    spec = spec_ref[...]
    kr, ki = spec[:, :LANES], spec[:, LANES:]
    prod = jnp.concatenate([dr * kr - di * ki, dr * ki + di * kr], axis=1)
    back = triple(halves(prod), (th[...], tl[...]))
    br, bi = back[:, :LANES], back[:, LANES:]
    cos, sin = tc[...], ts[...]
    turned = jnp.concatenate([br * cos - bi * sin, br * sin + bi * cos], axis=0)
    out_ref[...] = series + triple((gh[...], gl[...]), halves(turned))


def mlp_kernel(stack_ref, gain_ref, gate_ref, up_ref, down_ref, out_ref):
    channels = gate_ref.shape[0]
    each = stack_ref.shape[0] // channels
    residual = jnp.concatenate(
        [stack_ref[pl.ds(r, channels, stride=each), :].T for r in range(each)], axis=0
    )
    meansq = jnp.mean(residual * residual, axis=-1, keepdims=True)
    normed = (residual * lax.rsqrt(meansq + 1e-05) * gain_ref[...]).astype(bf16)
    gate = jnp.dot(normed, gate_ref[...], preferred_element_type=f32)
    upper = jnp.dot(normed, up_ref[...], preferred_element_type=f32)
    act = (gate / (1.0 + jnp.exp(-gate)) * upper).astype(bf16)
    out_ref[...] = (
        residual + jnp.dot(act, down_ref[...], preferred_element_type=f32)
    ).astype(bf16)


def per_device(spikes, read_in, kernel, gain, w_gate, w_up, w_down):
    time_groups = lax.axis_size("tm")
    neuron_groups = lax.axis_size("nrn")
    devices = time_groups * neuron_groups
    session = spikes.shape[0] * time_groups
    rows = session // LANES
    padded, first, twist_cos, twist_sin, second, third, fourth = dft_tables(rows)
    twist = (jnp.asarray(twist_cos, f32), jnp.asarray(twist_sin, f32))
    ahead = (*split(first), *twist, *split(second))
    core = (lax.axis_index("nrn") % 2).astype(jnp.int32).reshape(1)
    spikes, read_in = (
        pltpu.with_memory_space_constraint(x, pltpu.HBM) for x in (spikes, read_in)
    )
    swap = lambda x: lax.ppermute(x, "nrn", [(j, j ^ 1) for j in range(neuron_groups)])
    own, swapped, own_rest, swapped_rest = project(core, spikes, read_in, swap)
    spec = pl.pallas_call(
        lambda *refs: spectrum_kernel(*refs, padded=padded, scale=1.0 / session),
        out_shape=jax.ShapeDtypeStruct((padded, 2 * LANES), f32),
        compiler_params=pltpu.CompilerParams(vmem_limit_bytes=8 << 20),
        name="spectrum",
    )(kernel.reshape(rows, LANES), *ahead)
    swapped_rest, spec = lax.optimization_barrier((swapped_rest, spec))
    summed = jnp.concatenate([own + swapped, own_rest + swapped_rest], axis=1)
    same = [[d for d in range(devices) if d % 2 == c][::-1] for c in range(2)]
    parts = lax.all_to_all(summed, ("tm", "nrn"), 0, 0, tiled=True, axis_index_groups=same)
    mixed = pl.pallas_call(
        lambda *refs: convolve_kernel(*refs, padded=padded, groups=time_groups),
        out_shape=jax.ShapeDtypeStruct((rows, LANES), f32),
        compiler_params=pltpu.CompilerParams(vmem_limit_bytes=12 << 20),
        name="convolve",
    )(parts, spec, *ahead, *split(third), *split(fourth))
    stacked = lax.all_to_all(
        mixed.reshape(devices, rows // devices, LANES), ("tm", "nrn"), 0, 0, tiled=True
    )
    return pl.pallas_call(
        mlp_kernel,
        out_shape=jax.ShapeDtypeStruct((rows * LANES // devices, gain.shape[0]), bf16),
        compiler_params=pltpu.CompilerParams(vmem_limit_bytes=12 << 20),
        name="mlp",
    )(stacked.reshape(rows, LANES), gain.reshape(1, -1), w_gate, w_up, w_down)


def solution(mesh):
    placed = (P("tm", "nrn"), P("nrn", None), P(("tm", "nrn"), None), P(), P(), P(), P())
    return jax.shard_map(
        per_device, mesh=mesh, in_specs=placed, out_specs=P(("tm", "nrn"), None), check_vma=False
    )
```

```python
import math

import jax
import jax.numpy as jnp
import numpy as np
from jax import lax
from jax.experimental import pallas as pl
from jax.experimental.pallas import tpu as pltpu
from jax.sharding import PartitionSpec as P

f32 = jnp.float32
bf16 = jnp.bfloat16
LANES = 128


def split(table):
    table = np.asarray(table, np.float32)
    high = table.astype(jnp.bfloat16)
    low = (table - high.astype(np.float32)).astype(jnp.bfloat16)
    return jnp.asarray(high), jnp.asarray(low)


def dft_tables(rows):
    half = rows // 2 + 1
    padded = -(-half // 8) * 8
    total = rows * LANES
    a = np.arange(padded)
    keep = (a < half).astype(np.float64)
    row = np.arange(rows)
    angle = 2 * math.pi * ((a[:, None] * row[None, :]) % rows) / rows
    first = np.concatenate([np.cos(angle), -np.sin(angle)]) * np.tile(keep, 2)[:, None]
    lane = np.arange(LANES)
    angle = 2 * math.pi * ((a[:, None] * lane[None, :]) % total) / total
    twist_cos, twist_sin = np.cos(angle), np.sin(angle)
    angle = 2 * math.pi * ((lane[:, None] * lane[None, :]) % LANES) / LANES
    cos, sin = np.cos(angle), np.sin(angle)
    second = np.block([[cos, -sin], [sin, cos]])
    third = np.block([[cos, sin], [-sin, cos]])
    weight = np.where((a == 0) | (a == rows // 2), 1.0, 2.0) * keep
    angle = 2 * math.pi * ((row[:, None] * a[None, :]) % rows) / rows
    fourth = np.concatenate([np.cos(angle) * weight, -np.sin(angle) * weight], axis=1)
    return padded, first, twist_cos, twist_sin, second, third, fourth


def triple(left, right):
    (lh, ll), (rh, rl) = left, right
    dot = lambda p, q: jnp.dot(p, q, preferred_element_type=f32)
    return dot(lh, rh) + (dot(lh, rl) + dot(ll, rh))


def halves(value):
    high = value.astype(bf16)
    return high, (value - high.astype(f32)).astype(bf16)


def forward(signal, refs, padded):
    first_h, first_l, tc, ts, second_h, second_l = refs
    outer = triple((first_h[...], first_l[...]), halves(signal))
    real, imag = outer[:padded], outer[padded:]
    cos, sin = tc[...], ts[...]
    turned = jnp.concatenate([real * cos + imag * sin, imag * cos - real * sin], axis=1)
    return triple(halves(turned), (second_h[...], second_l[...]))


def put(part, own_ref, other_ref, block):
    turned = part.T
    half = turned.shape[0] // 2
    own_ref[:, block, :] = turned[:half]
    other_ref[:, block, :] = turned[half:]


def products(spikes_ref, weight, rows, own_ref, other_ref, held):
    for row in rows:
        part = jnp.dot(spikes_ref[pl.ds(row, LANES)], weight[...], preferred_element_type=f32)
        if held is not None:
            put(held[0], own_ref, other_ref, held[1])
        held = (part, row // LANES)
    return held


def project_kernel(core_ref, spikes_hbm, read_hbm, own_ref, other_ref, rest_ref, weight_ref, *scratch, pieces):
    spikes_ref, read_ref, arrived, read_arrived = scratch
    width = read_ref.shape[1]
    half = width // 2
    starts = [sum(pieces[:i]) for i in range(len(pieces) + 1)]
    fetch_read = pltpu.make_async_copy(read_hbm, read_ref, read_arrived)
    fetch_read.start()
    fetches = [
        pltpu.make_async_copy(
            spikes_hbm.at[pl.ds(first, size)], spikes_ref.at[pl.ds(first, size)], arrived.at[i]
        )
        for i, (first, size) in enumerate(zip(starts, pieces))
    ]
    fetches.append(
        pltpu.make_async_copy(
            spikes_hbm.at[pl.ds(starts[-1], rest_ref.shape[0])], rest_ref, arrived.at[len(pieces)]
        )
    )
    for i, fetch in enumerate(fetches[:3]):
        fetch.start(priority=min(i, 1))
    fetch_read.wait()
    channel = lax.broadcasted_iota(jnp.int32, (width, width), 0)
    place = lax.broadcasted_iota(jnp.int32, (width, width), 1)
    late = (place >= half).astype(jnp.int32)
    core = core_ref[0]
    wanted = 2 * (half - 1 - (place - half * late)) + (core + late - 2 * core * late)
    pick = jnp.where(channel == wanted, 1.0, 0.0).astype(bf16)
    weight_ref[...] = jnp.dot(read_ref[...], pick, preferred_element_type=f32).astype(bf16)
    held = None
    for i, (first, size) in enumerate(zip(starts, pieces)):
        fetches[i].wait()
        if i + 3 < len(fetches):
            fetches[i + 3].start(priority=1)
        rows = range(first, first + size, LANES)
        held = products(spikes_ref, weight_ref, rows, own_ref, other_ref, held)
    put(held[0], own_ref, other_ref, held[1])
    fetches[-1].wait()


def rest_kernel(rest_ref, weight_ref, own_ref, other_ref):
    rows = range(0, rest_ref.shape[0], LANES)
    held = products(rest_ref, weight_ref, rows, own_ref, other_ref, None)
    put(held[0], own_ref, other_ref, held[1])


def project(core, spikes, read_in, swap):
    bins, neurons = spikes.shape
    width = read_in.shape[1]
    part = lambda rows: jax.ShapeDtypeStruct((width // 2, rows // LANES, LANES), f32)
    pieces = [bins // 8, bins // 4, bins // 4, bins // 8]
    head = sum(pieces)
    tail = bins - head
    vmem = pl.BlockSpec(memory_space=pltpu.VMEM)
    own, other, rest, weight = pl.pallas_call(
        lambda *refs: project_kernel(*refs, pieces=pieces),
        out_shape=(
            part(head),
            part(head),
            jax.ShapeDtypeStruct((tail, neurons), bf16),
            jax.ShapeDtypeStruct((neurons, width), bf16),
        ),
        in_specs=[
            pl.BlockSpec(memory_space=pltpu.SMEM),
            pl.BlockSpec(memory_space=pltpu.HBM),
            pl.BlockSpec(memory_space=pltpu.HBM),
        ],
        out_specs=(vmem,) * 4,
        scratch_shapes=[
            pltpu.VMEM((head, neurons), bf16),
            pltpu.VMEM((neurons, width), bf16),
            pltpu.SemaphoreType.DMA((len(pieces) + 1,)),
            pltpu.SemaphoreType.DMA,
        ],
        compiler_params=pltpu.CompilerParams(vmem_limit_bytes=24 << 20),
        name="project",
    )(core, spikes, read_in)
    swapped = swap(other)
    own_rest, other_rest = pl.pallas_call(
        rest_kernel,
        out_shape=(part(tail), part(tail)),
        compiler_params=pltpu.CompilerParams(vmem_limit_bytes=8 << 20),
        name="rest",
    )(rest, weight)
    return own, swapped, own_rest, swap(other_rest)


def spectrum_kernel(kern_ref, fh, fl, tc, ts, sh, sl, out_ref, *, padded, scale):
    out_ref[...] = forward(kern_ref[...], (fh, fl, tc, ts, sh, sl), padded) * scale


def convolve_kernel(
    parts_ref, spec_ref, fh, fl, tc, ts, sh, sl, th, tl, gh, gl, out_ref, *, padded, groups
):
    parts = parts_ref[...]
    each, lanes = parts.shape[1], parts.shape[2]
    members = parts.shape[0] // groups
    parts = parts.reshape(groups, members, each, lanes)
    series = parts[:, 0]
    for m in range(1, members):
        series = series + parts[:, m]
    series = jnp.concatenate([series[g] for g in reversed(range(groups))], axis=0)
    data = forward(series, (fh, fl, tc, ts, sh, sl), padded)
    dr, di = data[:, :LANES], data[:, LANES:]
    spec = spec_ref[...]
    kr, ki = spec[:, :LANES], spec[:, LANES:]
    prod = jnp.concatenate([dr * kr - di * ki, dr * ki + di * kr], axis=1)
    back = triple(halves(prod), (th[...], tl[...]))
    br, bi = back[:, :LANES], back[:, LANES:]
    cos, sin = tc[...], ts[...]
    turned = jnp.concatenate([br * cos - bi * sin, br * sin + bi * cos], axis=0)
    out_ref[...] = series + triple((gh[...], gl[...]), halves(turned))


def mlp_kernel(stack_ref, gain_ref, gate_ref, up_ref, down_ref, out_ref):
    channels = gate_ref.shape[0]
    each = stack_ref.shape[0] // channels
    residual = jnp.concatenate(
        [stack_ref[pl.ds(r, channels, stride=each), :].T for r in range(each)], axis=0
    )
    meansq = jnp.mean(residual * residual, axis=-1, keepdims=True)
    normed = (residual * lax.rsqrt(meansq + 1e-05) * gain_ref[...]).astype(bf16)
    gate = jnp.dot(normed, gate_ref[...], preferred_element_type=f32)
    upper = jnp.dot(normed, up_ref[...], preferred_element_type=f32)
    act = (gate / (1.0 + jnp.exp(-gate)) * upper).astype(bf16)
    out_ref[...] = (
        residual + jnp.dot(act, down_ref[...], preferred_element_type=f32)
    ).astype(bf16)


def per_device(spikes, read_in, kernel, gain, w_gate, w_up, w_down):
    time_groups = lax.axis_size("tm")
    neuron_groups = lax.axis_size("nrn")
    devices = time_groups * neuron_groups
    session = spikes.shape[0] * time_groups
    rows = session // LANES
    padded, first, twist_cos, twist_sin, second, third, fourth = dft_tables(rows)
    twist = (jnp.asarray(twist_cos, f32), jnp.asarray(twist_sin, f32))
    ahead = (*split(first), *twist, *split(second))
    core = (lax.axis_index("nrn") % 2).astype(jnp.int32).reshape(1)
    spikes, read_in = (
        pltpu.with_memory_space_constraint(x, pltpu.HBM) for x in (spikes, read_in)
    )
    swap = lambda x: lax.ppermute(x, "nrn", [(j, j ^ 1) for j in range(neuron_groups)])
    own, swapped, own_rest, swapped_rest = project(core, spikes, read_in, swap)
    spec = pl.pallas_call(
        lambda *refs: spectrum_kernel(*refs, padded=padded, scale=1.0 / session),
        out_shape=jax.ShapeDtypeStruct((padded, 2 * LANES), f32),
        compiler_params=pltpu.CompilerParams(vmem_limit_bytes=8 << 20),
        name="spectrum",
    )(kernel.reshape(rows, LANES), *ahead)
    swapped_rest, spec = lax.optimization_barrier((swapped_rest, spec))
    summed = jnp.concatenate([own, own_rest], axis=1) + jnp.concatenate([swapped, swapped_rest], axis=1)
    same = [[d for d in range(devices) if d % 2 == c][::-1] for c in range(2)]
    parts = lax.all_to_all(summed, ("tm", "nrn"), 0, 0, tiled=True, axis_index_groups=same)
    mixed = pl.pallas_call(
        lambda *refs: convolve_kernel(*refs, padded=padded, groups=time_groups),
        out_shape=jax.ShapeDtypeStruct((rows, LANES), f32),
        compiler_params=pltpu.CompilerParams(vmem_limit_bytes=12 << 20),
        name="convolve",
    )(parts, spec, *ahead, *split(third), *split(fourth))
    stacked = lax.all_to_all(
        mixed.reshape(devices, rows // devices, LANES), ("tm", "nrn"), 0, 0, tiled=True
    )
    return pl.pallas_call(
        mlp_kernel,
        out_shape=jax.ShapeDtypeStruct((rows * LANES // devices, gain.shape[0]), bf16),
        compiler_params=pltpu.CompilerParams(vmem_limit_bytes=12 << 20),
        name="mlp",
    )(stacked.reshape(rows, LANES), gain.reshape(1, -1), w_gate, w_up, w_down)


def solution(mesh):
    placed = (P("tm", "nrn"), P("nrn", None), P(("tm", "nrn"), None), P(), P(), P(), P())
    return jax.shard_map(
        per_device, mesh=mesh, in_specs=placed, out_specs=P(("tm", "nrn"), None), check_vma=False
    )
```

```python
import math

import jax
import jax.numpy as jnp
import numpy as np
from jax import lax
from jax.experimental import pallas as pl
from jax.experimental.pallas import tpu as pltpu
from jax.sharding import PartitionSpec as P

f32 = jnp.float32
bf16 = jnp.bfloat16
LANES = 128


def split(table):
    table = np.asarray(table, np.float32)
    high = table.astype(jnp.bfloat16)
    low = (table - high.astype(np.float32)).astype(jnp.bfloat16)
    return jnp.asarray(high), jnp.asarray(low)


def dft_tables(rows):
    half = rows // 2 + 1
    padded = -(-half // 8) * 8
    total = rows * LANES
    a = np.arange(padded)
    keep = (a < half).astype(np.float64)
    row = np.arange(rows)
    angle = 2 * math.pi * ((a[:, None] * row[None, :]) % rows) / rows
    first = np.concatenate([np.cos(angle), -np.sin(angle)]) * np.tile(keep, 2)[:, None]
    lane = np.arange(LANES)
    angle = 2 * math.pi * ((a[:, None] * lane[None, :]) % total) / total
    twist_cos, twist_sin = np.cos(angle), np.sin(angle)
    angle = 2 * math.pi * ((lane[:, None] * lane[None, :]) % LANES) / LANES
    cos, sin = np.cos(angle), np.sin(angle)
    second = np.block([[cos, -sin], [sin, cos]])
    third = np.block([[cos, sin], [-sin, cos]])
    weight = np.where((a == 0) | (a == rows // 2), 1.0, 2.0) * keep
    angle = 2 * math.pi * ((row[:, None] * a[None, :]) % rows) / rows
    fourth = np.concatenate([np.cos(angle) * weight, -np.sin(angle) * weight], axis=1)
    return padded, first, twist_cos, twist_sin, second, third, fourth


def triple(left, right):
    (lh, ll), (rh, rl) = left, right
    dot = lambda p, q: jnp.dot(p, q, preferred_element_type=f32)
    return dot(lh, rh) + (dot(lh, rl) + dot(ll, rh))


def halves(value):
    high = value.astype(bf16)
    return high, (value - high.astype(f32)).astype(bf16)


def forward(signal, refs, padded):
    first_h, first_l, tc, ts, second_h, second_l = refs
    outer = triple((first_h[...], first_l[...]), halves(signal))
    real, imag = outer[:padded], outer[padded:]
    cos, sin = tc[...], ts[...]
    turned = jnp.concatenate([real * cos + imag * sin, imag * cos - real * sin], axis=1)
    return triple(halves(turned), (second_h[...], second_l[...]))


def put(part, own_ref, other_ref, block):
    turned = part.T
    half = turned.shape[0] // 2
    own_ref[:, block, :] = turned[:half]
    other_ref[:, block, :] = turned[half:]


def products(spikes_ref, weight, rows, own_ref, other_ref, held):
    for row in rows:
        part = jnp.dot(spikes_ref[pl.ds(row, LANES)], weight[...], preferred_element_type=f32)
        if held is not None:
            put(held[0], own_ref, other_ref, held[1])
        held = (part, row // LANES)
    return held


def project_kernel(core_ref, spikes_hbm, read_hbm, own_ref, other_ref, rest_ref, weight_ref, *scratch, pieces, torus):
    spikes_ref, read_ref, arrived, read_arrived = scratch
    width = read_ref.shape[1]
    half = width // 2
    starts = [sum(pieces[:i]) for i in range(len(pieces) + 1)]
    fetch_read = pltpu.make_async_copy(read_hbm, read_ref, read_arrived)
    fetch_read.start()
    fetches = [
        pltpu.make_async_copy(
            spikes_hbm.at[pl.ds(first, size)], spikes_ref.at[pl.ds(first, size)], arrived.at[i]
        )
        for i, (first, size) in enumerate(zip(starts, pieces))
    ]
    fetches.append(
        pltpu.make_async_copy(
            spikes_hbm.at[pl.ds(starts[-1], rest_ref.shape[0])], rest_ref, arrived.at[len(pieces)]
        )
    )
    for i, fetch in enumerate(fetches[:3]):
        fetch.start(priority=min(i, 1))
    fetch_read.wait()
    channel = lax.broadcasted_iota(jnp.int32, (width, width), 0)
    place = lax.broadcasted_iota(jnp.int32, (width, width), 1)
    late = (place >= half).astype(jnp.int32)
    core = core_ref[0]
    chip = half - 1 - (place - half * late)
    ys, xs, zs = torus
    chip = chip % ys * (xs * zs) + chip // (zs * ys) * zs + chip // ys % zs
    wanted = 2 * chip + (core + late - 2 * core * late)
    pick = jnp.where(channel == wanted, 1.0, 0.0).astype(bf16)
    weight_ref[...] = jnp.dot(read_ref[...], pick, preferred_element_type=f32).astype(bf16)
    held = None
    for i, (first, size) in enumerate(zip(starts, pieces)):
        fetches[i].wait()
        if i + 3 < len(fetches):
            fetches[i + 3].start(priority=1)
        rows = range(first, first + size, LANES)
        held = products(spikes_ref, weight_ref, rows, own_ref, other_ref, held)
    put(held[0], own_ref, other_ref, held[1])
    fetches[-1].wait()


def rest_kernel(rest_ref, weight_ref, own_ref, other_ref):
    rows = range(0, rest_ref.shape[0], LANES)
    held = products(rest_ref, weight_ref, rows, own_ref, other_ref, None)
    put(held[0], own_ref, other_ref, held[1])


def project(core, spikes, read_in, swap, torus):
    bins, neurons = spikes.shape
    width = read_in.shape[1]
    part = lambda rows: jax.ShapeDtypeStruct((width // 2, rows // LANES, LANES), f32)
    pieces = [bins // 8, bins // 4, bins // 4, bins // 8]
    head = sum(pieces)
    tail = bins - head
    vmem = pl.BlockSpec(memory_space=pltpu.VMEM)
    own, other, rest, weight = pl.pallas_call(
        lambda *refs: project_kernel(*refs, pieces=pieces, torus=torus),
        out_shape=(
            part(head),
            part(head),
            jax.ShapeDtypeStruct((tail, neurons), bf16),
            jax.ShapeDtypeStruct((neurons, width), bf16),
        ),
        in_specs=[
            pl.BlockSpec(memory_space=pltpu.SMEM),
            pl.BlockSpec(memory_space=pltpu.HBM),
            pl.BlockSpec(memory_space=pltpu.HBM),
        ],
        out_specs=(vmem,) * 4,
        scratch_shapes=[
            pltpu.VMEM((head, neurons), bf16),
            pltpu.VMEM((neurons, width), bf16),
            pltpu.SemaphoreType.DMA((len(pieces) + 1,)),
            pltpu.SemaphoreType.DMA,
        ],
        compiler_params=pltpu.CompilerParams(vmem_limit_bytes=24 << 20),
        name="project",
    )(core, spikes, read_in)
    swapped = swap(other)
    own_rest, other_rest = pl.pallas_call(
        rest_kernel,
        out_shape=(part(tail), part(tail)),
        compiler_params=pltpu.CompilerParams(vmem_limit_bytes=8 << 20),
        name="rest",
    )(rest, weight)
    return own, swapped, own_rest, swap(other_rest)


def spectrum_kernel(kern_ref, fh, fl, tc, ts, sh, sl, out_ref, *, padded, scale):
    out_ref[...] = forward(kern_ref[...], (fh, fl, tc, ts, sh, sl), padded) * scale


def convolve_kernel(
    parts_ref, spec_ref, fh, fl, tc, ts, sh, sl, th, tl, gh, gl, out_ref, *, padded, split_tm, split_nrn
):
    each, lanes = parts_ref.shape[1:]
    (ys, x_his), (x_los, zs) = split_tm, split_nrn
    parts = parts_ref[...].reshape(x_his, x_los, zs, ys, each, lanes)
    blocks = []
    for y in range(ys):
        for x_hi in range(x_his):
            block = None
            for x_lo in range(x_los):
                for z in range(zs):
                    part = parts[x_his - 1 - x_hi, x_los - 1 - x_lo, zs - 1 - z, ys - 1 - y]
                    block = part if block is None else block + part
            blocks.append(block)
    series = jnp.concatenate(blocks, axis=0)
    data = forward(series, (fh, fl, tc, ts, sh, sl), padded)
    dr, di = data[:, :LANES], data[:, LANES:]
    spec = spec_ref[...]
    kr, ki = spec[:, :LANES], spec[:, LANES:]
    prod = jnp.concatenate([dr * kr - di * ki, dr * ki + di * kr], axis=1)
    back = triple(halves(prod), (th[...], tl[...]))
    br, bi = back[:, :LANES], back[:, LANES:]
    cos, sin = tc[...], ts[...]
    turned = jnp.concatenate([br * cos - bi * sin, br * sin + bi * cos], axis=0)
    out_ref[...] = series + triple((gh[...], gl[...]), halves(turned))


def mlp_kernel(stack_ref, gain_ref, gate_ref, up_ref, down_ref, out_ref):
    channels = gate_ref.shape[0]
    each = stack_ref.shape[0] // channels
    residual = jnp.concatenate(
        [stack_ref[pl.ds(r, channels, stride=each), :].T for r in range(each)], axis=0
    )
    meansq = jnp.mean(residual * residual, axis=-1, keepdims=True)
    normed = (residual * lax.rsqrt(meansq + 1e-05) * gain_ref[...]).astype(bf16)
    gate = jnp.dot(normed, gate_ref[...], preferred_element_type=f32)
    upper = jnp.dot(normed, up_ref[...], preferred_element_type=f32)
    act = (gate / (1.0 + jnp.exp(-gate)) * upper).astype(bf16)
    out_ref[...] = (
        residual + jnp.dot(act, down_ref[...], preferred_element_type=f32)
    ).astype(bf16)


def per_device(spikes, read_in, kernel, gain, w_gate, w_up, w_down):
    time_groups = lax.axis_size("tm")
    neuron_groups = lax.axis_size("nrn")
    devices = time_groups * neuron_groups
    session = spikes.shape[0] * time_groups
    rows = session // LANES
    padded, first, twist_cos, twist_sin, second, third, fourth = dft_tables(rows)
    twist = (jnp.asarray(twist_cos, f32), jnp.asarray(twist_sin, f32))
    ahead = (*split(first), *twist, *split(second))
    core = (lax.axis_index("nrn") % 2).astype(jnp.int32).reshape(1)
    spikes, read_in = (
        pltpu.with_memory_space_constraint(x, pltpu.HBM) for x in (spikes, read_in)
    )
    swap = lambda x: lax.ppermute(x, "nrn", [(j, j ^ 1) for j in range(neuron_groups)])
    split_tm = (time_groups // 2, 2)
    split_nrn = (2, neuron_groups // 4)
    ys, xs, zs = split_tm[0], split_tm[1] * split_nrn[0], split_nrn[1]
    own, swapped, own_rest, swapped_rest = project(core, spikes, read_in, swap, (ys, xs, zs))
    spec = pl.pallas_call(
        lambda *refs: spectrum_kernel(*refs, padded=padded, scale=1.0 / session),
        out_shape=jax.ShapeDtypeStruct((padded, 2 * LANES), f32),
        compiler_params=pltpu.CompilerParams(vmem_limit_bytes=8 << 20),
        name="spectrum",
    )(kernel.reshape(rows, LANES), *ahead)
    swapped_rest, spec = lax.optimization_barrier((swapped_rest, spec))
    summed = jnp.concatenate([own, own_rest], axis=1) + jnp.concatenate([swapped, swapped_rest], axis=1)
    chips = [(y * xs + x) * zs + z for x in range(xs) for z in range(zs) for y in range(ys)][::-1]
    same = [[2 * chip + c for chip in chips] for c in range(2)]
    parts = lax.all_to_all(summed, ("tm", "nrn"), 0, 0, tiled=True, axis_index_groups=same)
    mixed = pl.pallas_call(
        lambda *refs: convolve_kernel(
            *refs, padded=padded, split_tm=split_tm, split_nrn=split_nrn
        ),
        out_shape=jax.ShapeDtypeStruct((rows, LANES), f32),
        compiler_params=pltpu.CompilerParams(vmem_limit_bytes=12 << 20),
        name="convolve",
    )(parts, spec, *ahead, *split(third), *split(fourth))
    stacked = lax.all_to_all(
        mixed.reshape(devices, rows // devices, LANES), ("tm", "nrn"), 0, 0, tiled=True
    )
    return pl.pallas_call(
        mlp_kernel,
        out_shape=jax.ShapeDtypeStruct((rows * LANES // devices, gain.shape[0]), bf16),
        compiler_params=pltpu.CompilerParams(vmem_limit_bytes=12 << 20),
        name="mlp",
    )(stacked.reshape(rows, LANES), gain.reshape(1, -1), w_gate, w_up, w_down)


def solution(mesh):
    placed = (P("tm", "nrn"), P("nrn", None), P(("tm", "nrn"), None), P(), P(), P(), P())
    return jax.shard_map(
        per_device, mesh=mesh, in_specs=placed, out_specs=P(("tm", "nrn"), None), check_vma=False
    )
```

```python
import math

import jax
import jax.numpy as jnp
import numpy as np
from jax import lax
from jax.experimental import pallas as pl
from jax.experimental.pallas import tpu as pltpu
from jax.sharding import PartitionSpec as P

f32 = jnp.float32
bf16 = jnp.bfloat16
LANES = 128


def split(table):
    table = np.asarray(table, np.float32)
    high = table.astype(jnp.bfloat16)
    low = (table - high.astype(np.float32)).astype(jnp.bfloat16)
    return jnp.asarray(high), jnp.asarray(low)


def dft_tables(rows):
    half = rows // 2 + 1
    padded = -(-half // 8) * 8
    total = rows * LANES
    a = np.arange(padded)
    keep = (a < half).astype(np.float64)
    row = np.arange(rows)
    angle = 2 * math.pi * ((a[:, None] * row[None, :]) % rows) / rows
    first = np.concatenate([np.cos(angle), -np.sin(angle)]) * np.tile(keep, 2)[:, None]
    lane = np.arange(LANES)
    angle = 2 * math.pi * ((a[:, None] * lane[None, :]) % total) / total
    twist_cos, twist_sin = np.cos(angle), np.sin(angle)
    angle = 2 * math.pi * ((lane[:, None] * lane[None, :]) % LANES) / LANES
    cos, sin = np.cos(angle), np.sin(angle)
    second = np.block([[cos, -sin], [sin, cos]])
    third = np.block([[cos, sin], [-sin, cos]])
    weight = np.where((a == 0) | (a == rows // 2), 1.0, 2.0) * keep
    angle = 2 * math.pi * ((row[:, None] * a[None, :]) % rows) / rows
    fourth = np.concatenate([np.cos(angle) * weight, -np.sin(angle) * weight], axis=1)
    return padded, first, twist_cos, twist_sin, second, third, fourth


def triple(left, right):
    (lh, ll), (rh, rl) = left, right
    dot = lambda p, q: jnp.dot(p, q, preferred_element_type=f32)
    return dot(lh, rh) + (dot(lh, rl) + dot(ll, rh))


def halves(value):
    high = value.astype(bf16)
    return high, (value - high.astype(f32)).astype(bf16)


def forward(signal, refs, padded):
    first_h, first_l, tc, ts, second_h, second_l = refs
    outer = triple((first_h[...], first_l[...]), halves(signal))
    real, imag = outer[:padded], outer[padded:]
    cos, sin = tc[...], ts[...]
    turned = jnp.concatenate([real * cos + imag * sin, imag * cos - real * sin], axis=1)
    return triple(halves(turned), (second_h[...], second_l[...]))


def put(part, own_ref, other_ref, block):
    turned = part.T
    half = turned.shape[0] // 2
    own_ref[:, block, :] = turned[:half]
    other_ref[:, block, :] = turned[half:]


def products(spikes_ref, weight, rows, own_ref, other_ref, held):
    for row in rows:
        part = jnp.dot(spikes_ref[pl.ds(row, LANES)], weight[...], preferred_element_type=f32)
        if held is not None:
            put(held[0], own_ref, other_ref, held[1])
        held = (part, row // LANES)
    return held


def project_kernel(core_ref, spikes_hbm, read_hbm, own_ref, other_ref, rest_ref, weight_ref, *scratch, pieces, torus):
    spikes_ref, read_ref, arrived, read_arrived = scratch
    width = read_ref.shape[1]
    half = width // 2
    starts = [sum(pieces[:i]) for i in range(len(pieces) + 1)]
    fetch_read = pltpu.make_async_copy(read_hbm, read_ref, read_arrived)
    fetch_read.start()
    fetches = [
        pltpu.make_async_copy(
            spikes_hbm.at[pl.ds(first, size)], spikes_ref.at[pl.ds(first, size)], arrived.at[i]
        )
        for i, (first, size) in enumerate(zip(starts, pieces))
    ]
    fetches.append(
        pltpu.make_async_copy(
            spikes_hbm.at[pl.ds(starts[-1], rest_ref.shape[0])], rest_ref, arrived.at[len(pieces)]
        )
    )
    for i, fetch in enumerate(fetches[:4]):
        fetch.start(priority=min(i, 1))
    fetch_read.wait()
    channel = lax.broadcasted_iota(jnp.int32, (width, width), 0)
    place = lax.broadcasted_iota(jnp.int32, (width, width), 1)
    late = (place >= half).astype(jnp.int32)
    core = core_ref[0]
    chip = half - 1 - (place - half * late)
    ys, xs, zs = torus
    chip = chip % ys * (xs * zs) + chip // (zs * ys) * zs + chip // ys % zs
    wanted = 2 * chip + (core + late - 2 * core * late)
    pick = jnp.where(channel == wanted, 1.0, 0.0).astype(bf16)
    weight_ref[...] = jnp.dot(read_ref[...], pick, preferred_element_type=f32).astype(bf16)
    held = None
    for i, (first, size) in enumerate(zip(starts, pieces)):
        fetches[i].wait()
        if i + 4 < len(fetches):
            fetches[i + 4].start(priority=1)
        rows = range(first, first + size, LANES)
        held = products(spikes_ref, weight_ref, rows, own_ref, other_ref, held)
    put(held[0], own_ref, other_ref, held[1])
    fetches[-1].wait()


def rest_kernel(rest_ref, weight_ref, own_ref, other_ref):
    rows = range(0, rest_ref.shape[0], LANES)
    held = products(rest_ref, weight_ref, rows, own_ref, other_ref, None)
    put(held[0], own_ref, other_ref, held[1])


def project(core, spikes, read_in, swap, torus):
    bins, neurons = spikes.shape
    width = read_in.shape[1]
    part = lambda rows: jax.ShapeDtypeStruct((width // 2, rows // LANES, LANES), f32)
    pieces = [bins // 8, bins // 4, bins // 4, bins // 8]
    head = sum(pieces)
    tail = bins - head
    vmem = pl.BlockSpec(memory_space=pltpu.VMEM)
    own, other, rest, weight = pl.pallas_call(
        lambda *refs: project_kernel(*refs, pieces=pieces, torus=torus),
        out_shape=(
            part(head),
            part(head),
            jax.ShapeDtypeStruct((tail, neurons), bf16),
            jax.ShapeDtypeStruct((neurons, width), bf16),
        ),
        in_specs=[
            pl.BlockSpec(memory_space=pltpu.SMEM),
            pl.BlockSpec(memory_space=pltpu.HBM),
            pl.BlockSpec(memory_space=pltpu.HBM),
        ],
        out_specs=(vmem,) * 4,
        scratch_shapes=[
            pltpu.VMEM((head, neurons), bf16),
            pltpu.VMEM((neurons, width), bf16),
            pltpu.SemaphoreType.DMA((len(pieces) + 1,)),
            pltpu.SemaphoreType.DMA,
        ],
        compiler_params=pltpu.CompilerParams(vmem_limit_bytes=24 << 20),
        name="project",
    )(core, spikes, read_in)
    swapped = swap(other)
    own_rest, other_rest = pl.pallas_call(
        rest_kernel,
        out_shape=(part(tail), part(tail)),
        compiler_params=pltpu.CompilerParams(vmem_limit_bytes=8 << 20),
        name="rest",
    )(rest, weight)
    return own, swapped, own_rest, swap(other_rest)


def spectrum_kernel(kern_ref, fh, fl, tc, ts, sh, sl, out_ref, *, padded, scale):
    out_ref[...] = forward(kern_ref[...], (fh, fl, tc, ts, sh, sl), padded) * scale


def convolve_kernel(
    parts_ref, spec_ref, fh, fl, tc, ts, sh, sl, th, tl, gh, gl, out_ref, *, padded, split_tm, split_nrn
):
    each, lanes = parts_ref.shape[1:]
    (ys, x_his), (x_los, zs) = split_tm, split_nrn
    parts = parts_ref[...].reshape(x_his, x_los, zs, ys, each, lanes)
    blocks = []
    for y in range(ys):
        for x_hi in range(x_his):
            block = None
            for x_lo in range(x_los):
                for z in range(zs):
                    part = parts[x_his - 1 - x_hi, x_los - 1 - x_lo, zs - 1 - z, ys - 1 - y]
                    block = part if block is None else block + part
            blocks.append(block)
    series = jnp.concatenate(blocks, axis=0)
    data = forward(series, (fh, fl, tc, ts, sh, sl), padded)
    dr, di = data[:, :LANES], data[:, LANES:]
    spec = spec_ref[...]
    kr, ki = spec[:, :LANES], spec[:, LANES:]
    prod = jnp.concatenate([dr * kr - di * ki, dr * ki + di * kr], axis=1)
    back = triple(halves(prod), (th[...], tl[...]))
    br, bi = back[:, :LANES], back[:, LANES:]
    cos, sin = tc[...], ts[...]
    turned = jnp.concatenate([br * cos - bi * sin, br * sin + bi * cos], axis=0)
    out_ref[...] = series + triple((gh[...], gl[...]), halves(turned))


def mlp_kernel(stack_ref, gain_ref, gate_ref, up_ref, down_ref, out_ref):
    channels = gate_ref.shape[0]
    each = stack_ref.shape[0] // channels
    residual = jnp.concatenate(
        [stack_ref[pl.ds(r, channels, stride=each), :].T for r in range(each)], axis=0
    )
    meansq = jnp.mean(residual * residual, axis=-1, keepdims=True)
    normed = (residual * lax.rsqrt(meansq + 1e-05) * gain_ref[...]).astype(bf16)
    gate = jnp.dot(normed, gate_ref[...], preferred_element_type=f32)
    upper = jnp.dot(normed, up_ref[...], preferred_element_type=f32)
    act = (gate / (1.0 + jnp.exp(-gate)) * upper).astype(bf16)
    out_ref[...] = (
        residual + jnp.dot(act, down_ref[...], preferred_element_type=f32)
    ).astype(bf16)


def per_device(spikes, read_in, kernel, gain, w_gate, w_up, w_down):
    time_groups = lax.axis_size("tm")
    neuron_groups = lax.axis_size("nrn")
    devices = time_groups * neuron_groups
    session = spikes.shape[0] * time_groups
    rows = session // LANES
    padded, first, twist_cos, twist_sin, second, third, fourth = dft_tables(rows)
    twist = (jnp.asarray(twist_cos, f32), jnp.asarray(twist_sin, f32))
    ahead = (*split(first), *twist, *split(second))
    core = (lax.axis_index("nrn") % 2).astype(jnp.int32).reshape(1)
    spikes, read_in = (
        pltpu.with_memory_space_constraint(x, pltpu.HBM) for x in (spikes, read_in)
    )
    swap = lambda x: lax.ppermute(x, "nrn", [(j, j ^ 1) for j in range(neuron_groups)])
    split_tm = (time_groups // 2, 2)
    split_nrn = (2, neuron_groups // 4)
    ys, xs, zs = split_tm[0], split_tm[1] * split_nrn[0], split_nrn[1]
    own, swapped, own_rest, swapped_rest = project(core, spikes, read_in, swap, (ys, xs, zs))
    spec = pl.pallas_call(
        lambda *refs: spectrum_kernel(*refs, padded=padded, scale=1.0 / session),
        out_shape=jax.ShapeDtypeStruct((padded, 2 * LANES), f32),
        compiler_params=pltpu.CompilerParams(vmem_limit_bytes=8 << 20),
        name="spectrum",
    )(kernel.reshape(rows, LANES), *ahead)
    swapped_rest, spec = lax.optimization_barrier((swapped_rest, spec))
    summed = jnp.concatenate([own, own_rest], axis=1) + jnp.concatenate([swapped, swapped_rest], axis=1)
    chips = [(y * xs + x) * zs + z for x in range(xs) for z in range(zs) for y in range(ys)][::-1]
    same = [[2 * chip + c for chip in chips] for c in range(2)]
    parts = lax.all_to_all(summed, ("tm", "nrn"), 0, 0, tiled=True, axis_index_groups=same)
    mixed = pl.pallas_call(
        lambda *refs: convolve_kernel(
            *refs, padded=padded, split_tm=split_tm, split_nrn=split_nrn
        ),
        out_shape=jax.ShapeDtypeStruct((rows, LANES), f32),
        compiler_params=pltpu.CompilerParams(vmem_limit_bytes=12 << 20),
        name="convolve",
    )(parts, spec, *ahead, *split(third), *split(fourth))
    stacked = lax.all_to_all(
        mixed.reshape(devices, rows // devices, LANES), ("tm", "nrn"), 0, 0, tiled=True
    )
    return pl.pallas_call(
        mlp_kernel,
        out_shape=jax.ShapeDtypeStruct((rows * LANES // devices, gain.shape[0]), bf16),
        compiler_params=pltpu.CompilerParams(vmem_limit_bytes=12 << 20),
        name="mlp",
    )(stacked.reshape(rows, LANES), gain.reshape(1, -1), w_gate, w_up, w_down)


def solution(mesh):
    placed = (P("tm", "nrn"), P("nrn", None), P(("tm", "nrn"), None), P(), P(), P(), P())
    return jax.shard_map(
        per_device, mesh=mesh, in_specs=placed, out_specs=P(("tm", "nrn"), None), check_vma=False
    )
```
